256 devices in a mesh: sec: 8 (over y, core), op: 32 (over z, x).
Axes of the slice: x: 4, y: 4, z: 8, core: 2. Of those that a mesh axis runs over, the one named last changes fastest.
Arguments:
- wavefunction: bfloat16 [8, 512, 1024], P('sec', 'op'), may hold values from -4.5 to 4.5
- op_blocks: bfloat16 [32, 8, 1024, 1024], P('op', 'sec'), may hold values from -6 to 6
- basis_guess: bfloat16 [8, 1024, 512], P('sec'), may hold values from -4.5 to 4.5
- sector_sizes: int32 [8], replicated, may hold values from 768 to 1024
- kept_counts: int32 [8], replicated, may hold values from 256 to 512
- target_map: int32 [32, 8], replicated, may hold values from 0 to 7, as said below
- noise_numerator: int32 [1], replicated, may hold values from 256 to 1024
- noise_denominator: int32 [1], replicated, may hold values from 4194304 to 8388608
Outputs:
- kept_basis: float32 [8, 1024, 512], P('sec', 'op')
- rotated: float32 [32, 8, 512, 512], P('op', 'sec')
The draws below stay inside these ranges and needn't reach their ends.
Inputs may be any that keep to these rules, and one draw needn't show every extreme that they name: For every operator k, target_map[k] is a permutation of the 8 sectors.
All inputs are finite; a program needn't handle non-finite values.
Results may differ from the reference program's by a relative error of at most 0.005.
Values may be sent and summed in bfloat16 or wider, within the bound.
No kernel may reach another device: no remote copies, remote signals or barrier semaphores. Data moves between devices by JAX's collectives and lax.ppermute only.
A program may use at most 64 MiB of HBM per device.

```python
import jax
import jax.numpy as jnp
from jax import lax

DIM = 1024
KEEP = 512
COLS = 512
SECTORS = 8
OPS = 32


def draw_target_map(key, part):
    operator_keys = jax.random.split(jax.random.fold_in(key, 17), OPS)
    orders = jax.vmap(lambda operator_key: jax.random.permutation(operator_key, SECTORS))(operator_keys)
    return orders.astype(jnp.int32)


def rough_rows(key, shape):
    values = jax.random.normal(jax.random.fold_in(key, 3), shape, jnp.float32)
    return jnp.clip(values, -4.5, 4.5)


def draw_wavefunction(key, part):
    return rough_rows(jax.random.fold_in(key, 29), (SECTORS, COLS, DIM)).astype(jnp.bfloat16)


def draw_basis_guess(key, part):
    return rough_rows(jax.random.fold_in(key, 31), (SECTORS, DIM, KEEP)).astype(jnp.bfloat16)


def set_ends(result, stream_key, least, high):
    spot = [jax.random.randint(jax.random.fold_in(stream_key, axis), (), 0, length) for axis, length in enumerate(result.shape)]
    widest = result.shape.index(max(result.shape))
    beside = spot[:widest] + [(spot[widest] + 1) % result.shape[widest]] + spot[widest + 1:]
    return result.at[tuple(spot)].set(least).at[tuple(beside)].set(high)


def block_levels(own_key, extent, pieces, smallest, top_value):
    loudness = 1.0
    for dim, parts in pieces:
        steps = jax.random.uniform(jax.random.fold_in(jax.random.fold_in(own_key, 6), dim), (parts,), jnp.float32, smallest / len(pieces), top_value / len(pieces))
        loudness = loudness * jnp.repeat(jnp.exp(steps), extent[dim] // parts).reshape((-1,) + (1,) * (len(extent) - 1 - dim))
    return loudness


def normal_values(own_key, dims, spread, bound, pieces=(), kind=jnp.bfloat16):
    values = spread * jax.random.normal(own_key, dims, jnp.float32)
    if pieces:
        values = values * block_levels(own_key, dims, pieces, -0.22, 0.18)
    return jnp.clip(values, -bound, bound).astype(kind)


def setup_inputs(seed: int = 0) -> dict:
    splits = jax.random.split(jax.random.key(seed), 9)
    return {
        "wavefunction": draw_wavefunction(jax.random.fold_in(splits[8], 71), 0),
        "op_blocks": normal_values(splits[1], (OPS, SECTORS, DIM, DIM), 1.0, 6.0, ((0, 32), (1, 8))),
        "basis_guess": draw_basis_guess(jax.random.fold_in(splits[8], 71), 0),
        "sector_sizes": set_ends(jax.random.randint(splits[3], (SECTORS,), 3 * DIM // 4, DIM + 1), jax.random.fold_in(splits[3], 1), 3 * DIM // 4, DIM).astype(jnp.int32),
        "kept_counts": set_ends(jax.random.randint(splits[4], (SECTORS,), KEEP // 2, KEEP + 1), jax.random.fold_in(splits[4], 1), KEEP // 2, KEEP).astype(jnp.int32),
        "target_map": draw_target_map(jax.random.fold_in(splits[8], 71), 0),
        "noise_numerator": jax.random.randint(splits[6], (1,), 256, 1025).astype(jnp.int32),
        "noise_denominator": jax.random.randint(splits[7], (1,), 4096 * DIM, 8192 * DIM + 1).astype(jnp.int32),
    }


def source_sectors(target_map):
    sectors = jnp.arange(SECTORS, dtype=jnp.int32)
    matches = target_map[:, :, None] == sectors[None, None, :]
    return jnp.sum(jnp.where(matches, sectors[None, :, None], 0), axis=1).astype(jnp.int32)

def reference(wavefunction, op_blocks, basis_guess, sector_sizes, kept_counts, target_map, noise_numerator, noise_denominator):
    highest = lax.Precision.HIGHEST
    noise_weight = noise_numerator[0].astype(jnp.float32) / noise_denominator[0].astype(jnp.float32)
    sources = source_sectors(target_map)
    states = jnp.arange(DIM, dtype=jnp.int32)
    state_mask = states[None, :] < sector_sizes[:, None]
    kept_mask = jnp.arange(KEEP, dtype=jnp.int32)[None, :] < kept_counts[:, None]
    masked = jnp.where(state_mask[:, None, :], wavefunction, jnp.zeros((), wavefunction.dtype))
    masked_wide = masked.astype(jnp.float32)
    base = jnp.einsum('scx,scy->sxy', masked_wide, masked_wide, precision=highest)

    def add_operator(running, inputs):
        blocks, anchor = inputs
        moved = jnp.take(masked_wide, anchor, axis=0)
        perturbed = jnp.einsum('tcx,txy->tcy', moved, blocks.astype(jnp.float32), precision=highest)
        perturbed = lax.optimization_barrier(perturbed.astype(jnp.bfloat16)).astype(jnp.float32)
        return (running + jnp.einsum('tcx,tcy->txy', perturbed, perturbed, precision=highest), None)
    noise_sum, unused = lax.scan(add_operator, jnp.zeros_like(base), (op_blocks, sources))
    density = base + noise_weight * noise_sum
    guess_masked = jnp.where(state_mask[:, :, None], basis_guess, jnp.zeros((), basis_guess.dtype)).astype(jnp.float32)
    image = jnp.einsum('sxy,syk->sxk', density, guess_masked, precision=highest)
    image = jnp.where(state_mask[:, :, None] & kept_mask[:, None, :], image, jnp.float32(0.0))
    padding = jnp.where(kept_mask, jnp.float32(0.0), jnp.float32(1.0))
    correlation = jnp.einsum('sdk,sdm->skm', image, image, precision=highest) + padding[:, :, None] * jnp.eye(KEEP, dtype=jnp.float32)[None]
    factor = jnp.linalg.cholesky(correlation)
    new_basis = lax.linalg.triangular_solve(factor, image, left_side=False, lower=True, transpose_a=True)
    kept_basis = new_basis * DIM ** 0.5
    basis_wide = lax.optimization_barrier(new_basis.astype(jnp.bfloat16)).astype(jnp.float32)

    def rotate(inputs):
        blocks, anchor = inputs
        mapped = jnp.einsum('txy,tyk->txk', blocks.astype(jnp.float32), basis_wide, precision=highest)
        mapped = lax.optimization_barrier(mapped.astype(jnp.bfloat16)).astype(jnp.float32)
        return jnp.einsum('txk,txm->tkm', jnp.take(basis_wide, anchor, axis=0), mapped, precision=highest)
    rotated = lax.map(rotate, (op_blocks, sources))
    return (kept_basis, rotated)
```

```python
import jax
import jax.numpy as jnp
from jax import lax
from jax.experimental import pallas as pl
from jax.experimental.pallas import tpu as pltpu
from jax.sharding import PartitionSpec as P

HI = lax.Precision.HIGHEST
LANE = 128

def dot(a, b, ca, cb):
    return lax.dot_general(a, b, (((ca,), (cb,)), ((), ())), precision=HI,
                           preferred_element_type=jnp.float32)

def factor_block(block):
    n = LANE
    sub = lax.broadcasted_iota(jnp.int32, (8, LANE), 0)
    lane = lax.broadcasted_iota(jnp.int32, (8, LANE), 1)
    groups = n // 8
    per = 4
    rows = [block[8 * g:8 * g + 8, :] for g in range(groups)]
    aug = [jnp.where(lane == sub + 8 * g, 1.0, 0.0).astype(jnp.float32) for g in range(groups)]
    out = []
    for s in range(0, groups, per):
        done_r, done_w = [], []
        for g in range(s, s + per):
            v, w = rows[g], aug[g]
            cols = [jnp.broadcast_to(v[:, 8 * g + j:8 * g + j + 1], (8, LANE)) for j in range(8)]
            e = {(i, j): jnp.broadcast_to(cols[j][i:i + 1, :], (8, LANE)) for j in range(8) for i in range(j, 8)}
            inv, low = [], {}
            for j in range(8):
                d = e[j, j]
                r = lax.rsqrt(d)
                r = r * (1.5 - 0.5 * d * r * r)
                inv.append(r)
                for i in range(j + 1, 8):
                    low[i, j] = e[i, j] * r
                for k in range(j + 1, 8):
                    for i in range(k, 8):
                        e[i, k] = e[i, k] - low[i, j] * low[k, j]
            m = {}
            for c in range(8):
                m[c, c] = inv[c]
                for i in range(c + 1, 8):
                    t = low[i, c] * m[c, c]
                    for k in range(c + 1, i):
                        t = t + low[i, k] * m[k, c]
                    m[i, c] = -t * inv[i]
            rv = rw = None
            mcols = []
            for j in range(8):
                mc = jnp.zeros((8, LANE), jnp.float32)
                for i in range(j, 8):
                    mc = jnp.where(sub == i, m[i, j], mc)
                tv = mc * jnp.broadcast_to(v[j:j + 1, :], (8, LANE))
                tw = mc * jnp.broadcast_to(w[j:j + 1, :], (8, LANE))
                rv = tv if rv is None else rv + tv
                rw = tw if rw is None else rw + tw
            out.append(rw)
            done_r.append(rv)
            done_w.append(rw)
            if g + 1 < s + per:
                rvb = [jnp.broadcast_to(rv[j:j + 1, :], (8, LANE)) for j in range(8)]
                rwb = [jnp.broadcast_to(rw[j:j + 1, :], (8, LANE)) for j in range(8)]
                for h in range(g + 1, s + per):
                    raw = [jnp.broadcast_to(rows[h][:, 8 * g + j:8 * g + j + 1], (8, LANE)) for j in range(8)]
                    nv, nw = rows[h], aug[h]
                    for i in range(8):
                        f = raw[0] * m[i, 0]
                        for k in range(1, i + 1):
                            f = f + raw[k] * m[i, k]
                        nv = nv - f * rvb[i]
                        nw = nw - f * rwb[i]
                    rows[h], aug[h] = nv, nw
        if s + per < groups:
            left = jnp.concatenate(done_r, axis=0)
            both = jnp.concatenate([left, jnp.concatenate(done_w, axis=0)], axis=1)
            rest = 8 * (s + per)
            delta = dot(left, both, 0, 0)
            for h in range(s + per, groups):
                rows[h] = rows[h] - delta[8 * h:8 * h + 8, :LANE]
                aug[h] = aug[h] - delta[8 * h:8 * h + 8, LANE:]
    return jnp.concatenate(out, axis=0)


def orthogonalize_kernel(kept_ref, corr_ref, image_ref, tile_ref, half_ref, kept_tile_ref, a_ref, q_ref, t_ref):
    n = corr_ref.shape[0]
    blocks = n // LANE
    kept = kept_ref[0]
    r_i = lax.broadcasted_iota(jnp.int32, (n, n), 0)
    c_i = lax.broadcasted_iota(jnp.int32, (n, n), 1)
    a_ref[...] = corr_ref[...] + jnp.where((r_i == c_i) & (c_i >= kept), 1.0, 0.0)
    scale = float(image_ref.shape[0]) ** 0.5
    for b in range(blocks):
        lo, hi = b * LANE, (b + 1) * LANE
        inv = factor_block(a_ref[lo:hi, lo:hi])
        for src, dst in ((image_ref, q_ref), (tile_ref, t_ref)):
            t = src[:, lo:hi]
            if b:
                t = t - dot(dst[:, :lo], a_ref[:lo, lo:hi], 1, 0)
            dst[:, lo:hi] = dot(t, inv, 1, 1)
        half_ref[:, lo:hi] = q_ref[:, lo:hi].astype(jnp.bfloat16)
        kept_tile_ref[:, lo:hi] = t_ref[:, lo:hi] * scale
        if b + 1 < blocks:
            r = dot(inv, a_ref[lo:hi, hi:], 1, 0)
            a_ref[lo:hi, hi:] = r
            for c in range(b + 1, blocks):
                cl = c * LANE
                a_ref[cl:cl + LANE, cl:] = a_ref[cl:cl + LANE, cl:] - dot(
                    r[:, cl - hi:cl - hi + LANE], r[:, cl - hi:], 0, 0)


def orthogonalize(corr, image, tile, kept):
    n = corr.shape[0]
    vmem = pl.BlockSpec(memory_space=pltpu.VMEM)
    return pl.pallas_call(
        orthogonalize_kernel,
        out_shape=(
            jax.ShapeDtypeStruct(image.shape, jnp.bfloat16),
            jax.ShapeDtypeStruct(tile.shape, jnp.float32),
        ),
        in_specs=[pl.BlockSpec(memory_space=pltpu.SMEM), vmem, vmem, vmem],
        out_specs=(vmem, vmem),
        scratch_shapes=[
            pltpu.VMEM((n, n), jnp.float32),
            pltpu.VMEM(image.shape, jnp.float32),
            pltpu.VMEM(tile.shape, jnp.float32),
        ],
        compiler_params=pltpu.CompilerParams(vmem_limit_bytes=40 << 20),
        name="orthogonalize",
    )(kept, corr, image, tile)


def from_everyone(value, axis):
    size = lax.axis_size(axis)
    return lax.all_to_all(
        jnp.broadcast_to(value[None], (size, *value.shape)), axis, 0, 0, tiled=True
    )


def laid_out(tiles, dim):
    dims = list(tiles.shape[1:])
    dims[dim] *= tiles.shape[0]
    return jnp.moveaxis(tiles, 0, dim).reshape(dims)


def collect(value, axis, dim):
    tiles = from_everyone(value, axis)
    return laid_out(tiles, dim)


def in_blocks(value, dim, size):
    before, after = (value.shape[:dim], value.shape[dim + 1 :])
    return jnp.moveaxis(value.reshape(*before, size, -1, *after), dim, 0)


def summed_on_arrival(value, axis, dim):
    size = lax.axis_size(axis)
    tiles = lax.all_to_all(in_blocks(value, dim, size), axis, 0, 0, tiled=True)
    return jnp.sum(tiles, axis=0)


def source_sectors(target_map):
    sectors = jnp.arange(target_map.shape[1], dtype=jnp.int32)
    matches = target_map[:, :, None] == sectors[None, None, :]
    return jnp.sum(jnp.where(matches, sectors[None, :, None], 0), axis=1)


def fetch_pieces(own_slice, wanted_all):
    everyone = collect(own_slice, "sec", 0)
    outgoing = jnp.take(everyone, wanted_all, axis=0)
    incoming = lax.all_to_all(outgoing, "op", split_axis=1, concat_axis=1, tiled=True)
    return incoming.reshape(
        incoming.shape[0], incoming.shape[1] * incoming.shape[2], incoming.shape[3]
    )


def body(
    wavefunction,
    op_blocks,
    basis_guess,
    sector_sizes,
    kept_counts,
    target_map,
    noise_numerator,
    noise_denominator,
):
    highest = lax.Precision.HIGHEST
    local_count = wavefunction.shape[0]
    state_count = wavefunction.shape[2]
    kept_width = basis_guess.shape[2]
    tile_rows = state_count // lax.axis_size("op")
    sec_index = lax.axis_index("sec")
    op_index = lax.axis_index("op")
    noise_weight = noise_numerator[0].astype(jnp.float32) / noise_denominator[0].astype(jnp.float32)
    sources = source_sectors(target_map)
    own_sectors = sec_index * local_count + jnp.arange(local_count, dtype=jnp.int32)
    wanted_all = jnp.take(sources, own_sectors, axis=1).T
    wanted = lax.dynamic_index_in_dim(wanted_all, op_index, 1, keepdims=False)
    states = jnp.arange(state_count, dtype=jnp.int32)
    own_sizes = jnp.take(sector_sizes, own_sectors)
    own_mask = states[None, :] < own_sizes[:, None]
    source_mask = states[None, :] < jnp.take(sector_sizes, wanted)[:, None]
    own_kept = (
        jnp.arange(kept_width, dtype=jnp.int32)[None, :]
        < jnp.take(kept_counts, own_sectors)[:, None]
    )
    zero_half = jnp.zeros((), jnp.bfloat16)
    own_rows = jnp.where(own_mask[:, None, :], wavefunction, zero_half)
    moved = fetch_pieces(wavefunction, wanted_all)
    moved = jnp.where(source_mask[:, None, :], moved, zero_half)
    blocks = op_blocks[0]
    perturbed = jnp.einsum(
        "lcx,lxy->lcy", moved, blocks, preferred_element_type=jnp.float32
    ).astype(jnp.bfloat16)
    guess_rows = jnp.where(own_mask[:, :, None], basis_guess, zero_half)
    own_proj = jnp.einsum("lcx,lxk->lck", own_rows, guess_rows, preferred_element_type=jnp.float32)
    perturbed_proj = jnp.einsum(
        "lcx,lxk->lck", perturbed, guess_rows, preferred_element_type=jnp.float32
    )
    own_part = own_rows.astype(jnp.float32)
    perturbed_part = perturbed.astype(jnp.float32)
    contribution = jnp.einsum("lcr,lck->rlk", own_part, own_proj, precision=highest)
    image_rows = summed_on_arrival(
        contribution
        + noise_weight
        * jnp.einsum("lcr,lck->rlk", perturbed_part, perturbed_proj, precision=highest),
        "op",
        0,
    )
    image = jnp.transpose(image_rows, (1, 0, 2))
    row_ids = op_index * tile_rows + jnp.arange(tile_rows, dtype=jnp.int32)
    row_mask = row_ids[None, :] < own_sizes[:, None]
    image = jnp.where(row_mask[:, :, None] & own_kept[:, None, :], image, jnp.float32(0.0))
    full_image = collect(image, "op", 1)
    correlation = jnp.einsum("dk,dm->km", full_image[0], full_image[0], precision=highest)
    basis_half, kept_tile = orthogonalize(
        correlation, full_image[0], image[0], jnp.take(kept_counts, own_sectors)
    )
    basis_half = basis_half[None]
    kept_tile = kept_tile[None]
    mapped = jnp.einsum(
        "lxy,lyk->lxk", blocks, basis_half, preferred_element_type=jnp.float32
    ).astype(jnp.bfloat16)
    own_tile = lax.dynamic_slice_in_dim(basis_half, op_index * tile_rows, tile_rows, 1)
    source_basis = fetch_pieces(own_tile, wanted_all)
    rotated = jnp.einsum("lxk,lxm->lkm", source_basis, mapped, preferred_element_type=jnp.float32)
    return (kept_tile, rotated[None])


def solution(mesh):
    placed = (
        P("sec", "op", None),
        P("op", "sec", None, None),
        P("sec", None, None),
        P(),
        P(),
        P(),
        P(),
        P(),
    )
    return jax.shard_map(
        body,
        mesh=mesh,
        in_specs=placed,
        out_specs=(P("sec", "op", None), P("op", "sec", None, None)),
        check_vma=False,
    )
```

```python
import jax
import jax.numpy as jnp
from jax import lax
from jax.experimental import pallas as pl
from jax.experimental.pallas import tpu as pltpu
from jax.sharding import PartitionSpec as P

HIGHEST = lax.Precision.HIGHEST
LANE = 128
CUTS = (0, 512)


def dot(a, b, ca, cb):
    return lax.dot_general(
        a, b, (((ca,), (cb,)), ((), ())), precision=HIGHEST, preferred_element_type=jnp.float32
    )


def factor_block(block):
    n = LANE
    sub = lax.broadcasted_iota(jnp.int32, (8, LANE), 0)
    lane = lax.broadcasted_iota(jnp.int32, (8, LANE), 1)
    groups = n // 8
    per = 4
    rows = [block[8 * g:8 * g + 8, :] for g in range(groups)]
    aug = [jnp.where(lane == sub + 8 * g, 1.0, 0.0).astype(jnp.float32) for g in range(groups)]
    out = []
    for s in range(0, groups, per):
        done_r, done_w = [], []
        for g in range(s, s + per):
            v, w = rows[g], aug[g]
            cols = [jnp.broadcast_to(v[:, 8 * g + j:8 * g + j + 1], (8, LANE)) for j in range(8)]
            e = {(i, j): jnp.broadcast_to(cols[j][i:i + 1, :], (8, LANE)) for j in range(8) for i in range(j, 8)}
            inv, low = [], {}
            for j in range(8):
                d = e[j, j]
                r = lax.rsqrt(d)
                r = r * (1.5 - 0.5 * d * r * r)
                inv.append(r)
                for i in range(j + 1, 8):
                    low[i, j] = e[i, j] * r
                for k in range(j + 1, 8):
                    for i in range(k, 8):
                        e[i, k] = e[i, k] - low[i, j] * low[k, j]
            m = {}
            for c in range(8):
                m[c, c] = inv[c]
                for i in range(c + 1, 8):
                    t = low[i, c] * m[c, c]
                    for k in range(c + 1, i):
                        t = t + low[i, k] * m[k, c]
                    m[i, c] = -t * inv[i]
            rv = rw = None
            mcols = []
            for j in range(8):
                mc = jnp.zeros((8, LANE), jnp.float32)
                for i in range(j, 8):
                    mc = jnp.where(sub == i, m[i, j], mc)
                tv = mc * jnp.broadcast_to(v[j:j + 1, :], (8, LANE))
                tw = mc * jnp.broadcast_to(w[j:j + 1, :], (8, LANE))
                rv = tv if rv is None else rv + tv
                rw = tw if rw is None else rw + tw
            out.append(rw)
            done_r.append(rv)
            done_w.append(rw)
            if g + 1 < s + per:
                rvb = [jnp.broadcast_to(rv[j:j + 1, :], (8, LANE)) for j in range(8)]
                rwb = [jnp.broadcast_to(rw[j:j + 1, :], (8, LANE)) for j in range(8)]
                for h in range(g + 1, s + per):
                    raw = [jnp.broadcast_to(rows[h][:, 8 * g + j:8 * g + j + 1], (8, LANE)) for j in range(8)]
                    nv, nw = rows[h], aug[h]
                    for i in range(8):
                        f = raw[0] * m[i, 0]
                        for k in range(1, i + 1):
                            f = f + raw[k] * m[i, k]
                        nv = nv - f * rvb[i]
                        nw = nw - f * rwb[i]
                    rows[h], aug[h] = nv, nw
        if s + per < groups:
            left = jnp.concatenate(done_r, axis=0)
            both = jnp.concatenate([left, jnp.concatenate(done_w, axis=0)], axis=1)
            rest = 8 * (s + per)
            delta = dot(left, both, 0, 0)
            for h in range(s + per, groups):
                rows[h] = rows[h] - delta[8 * h:8 * h + 8, :LANE]
                aug[h] = aug[h] - delta[8 * h:8 * h + 8, LANE:]
    return jnp.concatenate(out, axis=0)


def basis_kernel(offset, scalars_ref, image_ref, *refs):
    count = len(refs) - 6
    before = refs[:count]
    half_ref, tile_half_ref, kept_ref, q_ref, a_ref, t_ref = refs[count:]
    rows, width = image_ref.shape
    kept, own = scalars_ref[0], scalars_ref[1]
    if before:
        t_ref[...] = image_ref[...]
        for earlier in before:
            t_ref[...] = t_ref[...] - dot(
                earlier[...], dot(earlier[...], image_ref[...], 0, 0), 1, 0
            )
    else:
        t_ref[...] = image_ref[...]
    r_i = lax.broadcasted_iota(jnp.int32, (width, width), 0)
    c_i = lax.broadcasted_iota(jnp.int32, (width, width), 1)
    a_ref[...] = dot(t_ref[...], t_ref[...], 0, 0) + jnp.where(
        (r_i == c_i) & (c_i + offset >= kept), 1.0, 0.0
    )
    for lo in range(0, width, LANE):
        hi = lo + LANE
        inv = factor_block(a_ref[lo:hi, lo:hi])
        t = t_ref[:, lo:hi]
        if lo:
            t = t - dot(q_ref[:, :lo], a_ref[:lo, lo:hi], 1, 0)
        q = dot(t, inv, 1, 1)
        q_ref[:, lo:hi] = q
        half_ref[:, lo:hi] = q.astype(jnp.bfloat16)
        if hi < width:
            r = dot(inv, a_ref[lo:hi, hi:], 1, 0)
            a_ref[lo:hi, hi:] = r
            for c in range(hi, width, LANE):
                a_ref[c : c + LANE, c:] = a_ref[c : c + LANE, c:] - dot(
                    r[:, c - hi : c - hi + LANE], r[:, c - hi :], 0, 0
                )
    tile = kept_ref.shape[0]
    mine = q_ref[pl.ds(pl.multiple_of(own * tile, tile), tile), :]
    tile_half_ref[...] = mine.astype(jnp.bfloat16)
    kept_ref[...] = mine * float(rows) ** 0.5


def orthonormal(image, before, offset, scalars, tile):
    rows, width = image.shape
    vmem = pl.BlockSpec(memory_space=pltpu.VMEM)
    return pl.pallas_call(
        lambda *refs: basis_kernel(offset, *refs),
        out_shape=(
            jax.ShapeDtypeStruct((rows, width), jnp.bfloat16),
            jax.ShapeDtypeStruct((tile, width), jnp.bfloat16),
            jax.ShapeDtypeStruct((tile, width), jnp.float32),
            jax.ShapeDtypeStruct((rows, width), jnp.float32),
        ),
        in_specs=[pl.BlockSpec(memory_space=pltpu.SMEM)] + [vmem] * (1 + len(before)),
        out_specs=(vmem,) * 4,
        scratch_shapes=[
            pltpu.VMEM((width, width), jnp.float32),
            pltpu.VMEM((rows, width), jnp.float32),
        ],
        compiler_params=pltpu.CompilerParams(vmem_limit_bytes=40 << 20),
        cost_estimate=pl.CostEstimate(
            flops=40_000_000_000 * width // 512, bytes_accessed=rows * width * 12, transcendentals=0
        ),
        name="basis_%d" % offset,
    )(scalars, image, *before)


def from_everyone(value, axis):
    size = lax.axis_size(axis)
    return lax.all_to_all(
        jnp.broadcast_to(value[None], (size, *value.shape)), axis, 0, 0, tiled=True
    )


def source_sectors(target_map):
    sectors = jnp.arange(target_map.shape[1], dtype=jnp.int32)
    matches = target_map[:, :, None] == sectors[None, None, :]
    return jnp.sum(jnp.where(matches, sectors[None, :, None], 0), axis=1)


def fetch_pieces(own_slice, wanted_all):
    everyone = from_everyone(own_slice, "sec")
    outgoing = jnp.take(everyone, wanted_all, axis=0)
    incoming = lax.all_to_all(outgoing, "op", 0, 0, tiled=True)
    return incoming.reshape(-1, incoming.shape[-1])


def body(
    wavefunction,
    op_blocks,
    basis_guess,
    sector_sizes,
    kept_counts,
    target_map,
    noise_numerator,
    noise_denominator,
):
    state_count = wavefunction.shape[2]
    kept_width = basis_guess.shape[2]
    ops = lax.axis_size("op")
    tile_rows = state_count // ops
    sec_index = lax.axis_index("sec")
    op_index = lax.axis_index("op")
    noise_weight = noise_numerator[0].astype(jnp.float32) / noise_denominator[0].astype(jnp.float32)
    sources = source_sectors(target_map)
    wanted_all = jnp.take(sources, sec_index, axis=1)
    wanted = jnp.take(wanted_all, op_index)
    states = jnp.arange(state_count, dtype=jnp.int32)
    own_size = jnp.take(sector_sizes, sec_index)
    own_kept = jnp.take(kept_counts, sec_index)
    own_mask = states < own_size
    source_mask = states < jnp.take(sector_sizes, wanted)
    zero_half = jnp.zeros((), jnp.bfloat16)
    own_rows = jnp.where(own_mask[None, :], wavefunction[0], zero_half)
    moved = fetch_pieces(wavefunction[0], wanted_all)
    moved = jnp.where(source_mask[None, :], moved, zero_half)
    blocks = op_blocks[0, 0]
    perturbed = jnp.dot(moved, blocks, preferred_element_type=jnp.float32).astype(jnp.bfloat16)
    guess_rows = jnp.where(own_mask[:, None], basis_guess[0], zero_half)
    left = jnp.concatenate([perturbed, own_rows], axis=0)
    proj = jnp.dot(left, guess_rows, preferred_element_type=jnp.float32)
    is_noise = jnp.arange(left.shape[0]) < perturbed.shape[0]
    proj = proj * jnp.where(is_noise, noise_weight, jnp.float32(1.0))[:, None]
    proj_high = proj.astype(jnp.bfloat16)
    proj_low = (proj - proj_high.astype(jnp.float32)).astype(jnp.bfloat16)
    scalars = jnp.stack([own_kept, op_index])
    row_ids = op_index * tile_rows + jnp.arange(tile_rows, dtype=jnp.int32)
    row_mask = row_ids < own_size
    col_mask = jnp.arange(kept_width, dtype=jnp.int32) < own_kept
    cuts = list(zip(CUTS[:-1], CUTS[1:]))
    images = []
    sums = []
    for lo, hi in cuts:
        part = lax.dot_general(
            jnp.concatenate([left, left], axis=0),
            jnp.concatenate([proj_high[:, lo:hi], proj_low[:, lo:hi]], axis=0),
            (((0,), (0,)), ((), ())),
            preferred_element_type=jnp.float32,
        ).astype(jnp.bfloat16)
        tiles = lax.all_to_all(part.reshape(ops, tile_rows, hi - lo), "op", 0, 0, tiled=True)
        sums.append(jnp.sum(tiles.astype(jnp.float32), axis=0))
    for (lo, hi), total in zip(cuts, sums):
        image = jnp.where(row_mask[:, None] & col_mask[None, lo:hi], total, jnp.float32(0.0))
        images.append(from_everyone(image, "op").reshape(state_count, hi - lo))
    before, kept_tiles, mapped, fetched = [], [], [], []
    for (lo, hi), image in zip(cuts, images):
        half, tile_half, kept_tile, q = orthonormal(image, before, lo, scalars, tile_rows)
        before.append(q)
        kept_tiles.append(kept_tile)
        fetched.append(fetch_pieces(tile_half, wanted_all))
        mapped.append(
            jnp.dot(blocks, half, preferred_element_type=jnp.float32).astype(jnp.bfloat16)
        )
    mapped = jnp.concatenate(mapped, axis=1)
    rotated = jnp.concatenate(
        [
            lax.dot_general(
                source, mapped, (((0,), (0,)), ((), ())), preferred_element_type=jnp.float32
            )
            for source in fetched
        ],
        axis=0,
    )
    return (jnp.concatenate(kept_tiles, axis=1)[None], rotated[None, None])


def solution(mesh):
    placed = (
        P("sec", "op", None),
        P("op", "sec", None, None),
        P("sec", None, None),
        P(),
        P(),
        P(),
        P(),
        P(),
    )
    return jax.shard_map(
        body,
        mesh=mesh,
        in_specs=placed,
        out_specs=(P("sec", "op", None), P("op", "sec", None, None)),
        check_vma=False,
    )
```

```python
import jax
import jax.numpy as jnp
from jax import lax
from jax.experimental import pallas as pl
from jax.experimental.pallas import tpu as pltpu
from jax.sharding import PartitionSpec as P

HIGHEST = lax.Precision.HIGHEST
LANE = 128
CUTS = (0, 512)


def dot(a, b, ca, cb):
    return lax.dot_general(
        a, b, (((ca,), (cb,)), ((), ())), precision=HIGHEST, preferred_element_type=jnp.float32
    )


def factor_block(block):
    n = LANE
    sub = lax.broadcasted_iota(jnp.int32, (8, LANE), 0)
    lane = lax.broadcasted_iota(jnp.int32, (8, LANE), 1)
    groups = n // 8
    per = 4
    rows = [block[8 * g:8 * g + 8, :] for g in range(groups)]
    aug = [jnp.where(lane == sub + 8 * g, 1.0, 0.0).astype(jnp.float32) for g in range(groups)]
    out = []
    for s in range(0, groups, per):
        done_r, done_w = [], []
        for g in range(s, s + per):
            v, w = rows[g], aug[g]
            cols = [jnp.broadcast_to(v[:, 8 * g + j:8 * g + j + 1], (8, LANE)) for j in range(8)]
            e = {(i, j): jnp.broadcast_to(cols[j][i:i + 1, :], (8, LANE)) for j in range(8) for i in range(j, 8)}
            inv, low = [], {}
            for j in range(8):
                d = e[j, j]
                r = lax.rsqrt(d)
                r = r * (1.5 - 0.5 * d * r * r)
                inv.append(r)
                for i in range(j + 1, 8):
                    low[i, j] = e[i, j] * r
                for k in range(j + 1, 8):
                    for i in range(k, 8):
                        e[i, k] = e[i, k] - low[i, j] * low[k, j]
            m = {}
            for c in range(8):
                m[c, c] = inv[c]
                for i in range(c + 1, 8):
                    t = low[i, c] * m[c, c]
                    for k in range(c + 1, i):
                        t = t + low[i, k] * m[k, c]
                    m[i, c] = -t * inv[i]
            rv = rw = None
            mcols = []
            for j in range(8):
                mc = jnp.zeros((8, LANE), jnp.float32)
                for i in range(j, 8):
                    mc = jnp.where(sub == i, m[i, j], mc)
                tv = mc * jnp.broadcast_to(v[j:j + 1, :], (8, LANE))
                tw = mc * jnp.broadcast_to(w[j:j + 1, :], (8, LANE))
                rv = tv if rv is None else rv + tv
                rw = tw if rw is None else rw + tw
            out.append(rw)
            done_r.append(rv)
            done_w.append(rw)
            if g + 1 < s + per:
                rvb = [jnp.broadcast_to(rv[j:j + 1, :], (8, LANE)) for j in range(8)]
                rwb = [jnp.broadcast_to(rw[j:j + 1, :], (8, LANE)) for j in range(8)]
                for h in range(g + 1, s + per):
                    raw = [jnp.broadcast_to(rows[h][:, 8 * g + j:8 * g + j + 1], (8, LANE)) for j in range(8)]
                    nv, nw = rows[h], aug[h]
                    for i in range(8):
                        f = raw[0] * m[i, 0]
                        for k in range(1, i + 1):
                            f = f + raw[k] * m[i, k]
                        nv = nv - f * rvb[i]
                        nw = nw - f * rwb[i]
                    rows[h], aug[h] = nv, nw
        if s + per < groups:
            left = jnp.concatenate(done_r, axis=0)
            both = jnp.concatenate([left, jnp.concatenate(done_w, axis=0)], axis=1)
            rest = 8 * (s + per)
            delta = dot(left, both, 0, 0)
            for h in range(s + per, groups):
                rows[h] = rows[h] - delta[8 * h:8 * h + 8, :LANE]
                aug[h] = aug[h] - delta[8 * h:8 * h + 8, LANE:]
    return jnp.concatenate(out, axis=0)


def basis_kernel(offset, scalars_ref, image_ref, *refs):
    count = len(refs) - 6
    before = refs[:count]
    half_ref, tile_half_ref, kept_ref, q_ref, a_ref, t_ref = refs[count:]
    rows, width = image_ref.shape
    kept, own = scalars_ref[0], scalars_ref[1]
    if before:
        t_ref[...] = image_ref[...]
        for earlier in before:
            t_ref[...] = t_ref[...] - dot(
                earlier[...], dot(earlier[...], image_ref[...], 0, 0), 1, 0
            )
    else:
        t_ref[...] = image_ref[...]
    r_i = lax.broadcasted_iota(jnp.int32, (width, width), 0)
    c_i = lax.broadcasted_iota(jnp.int32, (width, width), 1)
    a_ref[...] = dot(t_ref[...], t_ref[...], 0, 0) + jnp.where(
        (r_i == c_i) & (c_i + offset >= kept), 1.0, 0.0
    )
    for lo in range(0, width, LANE):
        hi = lo + LANE
        inv = factor_block(a_ref[lo:hi, lo:hi])
        t = t_ref[:, lo:hi]
        if lo:
            t = t - dot(q_ref[:, :lo], a_ref[:lo, lo:hi], 1, 0)
        q = dot(t, inv, 1, 1)
        q_ref[:, lo:hi] = q
        half_ref[:, lo:hi] = q.astype(jnp.bfloat16)
        if hi < width:
            r = dot(inv, a_ref[lo:hi, hi:], 1, 0)
            a_ref[lo:hi, hi:] = r
            for c in range(hi, width, LANE):
                a_ref[c : c + LANE, c:] = a_ref[c : c + LANE, c:] - dot(
                    r[:, c - hi : c - hi + LANE], r[:, c - hi :], 0, 0
                )
    tile = kept_ref.shape[0]
    mine = q_ref[pl.ds(pl.multiple_of(own * tile, tile), tile), :]
    tile_half_ref[...] = mine.astype(jnp.bfloat16)
    kept_ref[...] = mine * float(rows) ** 0.5


def orthonormal(image, before, offset, scalars, tile):
    rows, width = image.shape
    vmem = pl.BlockSpec(memory_space=pltpu.VMEM)
    return pl.pallas_call(
        lambda *refs: basis_kernel(offset, *refs),
        out_shape=(
            jax.ShapeDtypeStruct((rows, width), jnp.bfloat16),
            jax.ShapeDtypeStruct((tile, width), jnp.bfloat16),
            jax.ShapeDtypeStruct((tile, width), jnp.float32),
            jax.ShapeDtypeStruct((rows, width), jnp.float32),
        ),
        in_specs=[pl.BlockSpec(memory_space=pltpu.SMEM)] + [vmem] * (1 + len(before)),
        out_specs=(vmem,) * 4,
        scratch_shapes=[
            pltpu.VMEM((width, width), jnp.float32),
            pltpu.VMEM((rows, width), jnp.float32),
        ],
        compiler_params=pltpu.CompilerParams(vmem_limit_bytes=40 << 20),
        cost_estimate=pl.CostEstimate(
            flops=40_000_000_000 * width // 512, bytes_accessed=rows * width * 12, transcendentals=0
        ),
        name="basis_%d" % offset,
    )(scalars, image, *before)


def from_everyone(value, axis):
    size = lax.axis_size(axis)
    return lax.all_to_all(
        jnp.broadcast_to(value[None], (size, *value.shape)), axis, 0, 0, tiled=True
    )


def source_sectors(target_map):
    sectors = jnp.arange(target_map.shape[1], dtype=jnp.int32)
    matches = target_map[:, :, None] == sectors[None, None, :]
    return jnp.sum(jnp.where(matches, sectors[None, :, None], 0), axis=1)


def gather_sectors(value):
    size = lax.axis_size("sec")
    other = lax.ppermute(value, "sec", [(i, i ^ 1) for i in range(size)])
    pair = jnp.stack([value, other])
    pairs = [pair] + [
        lax.ppermute(pair, "sec", [(i, (i + 2 * step) % size) for i in range(size)])
        for step in range(1, size // 2)
    ]
    return jnp.concatenate(pairs, axis=0)


def place_of(sector, own):
    chips = lax.axis_size("sec") // 2
    return (own // 2 - sector // 2 + chips) % chips * 2 + (own + sector) % 2


def fetch_pieces(own_slice, places):
    outgoing = jnp.take(gather_sectors(own_slice), places, axis=0, mode="clip")
    incoming = lax.all_to_all(outgoing, "op", 0, 0, tiled=True)
    return incoming.reshape(-1, incoming.shape[-1])


def in_halves(value):
    high = value.astype(jnp.bfloat16)
    return high, (value - high.astype(jnp.float32)).astype(jnp.bfloat16)


def from_left(left, high, low):
    return lax.dot_general(
        jnp.concatenate([left, left], axis=0),
        jnp.concatenate([high, low], axis=0),
        (((0,), (0,)), ((), ())),
        preferred_element_type=jnp.float32,
    )


def body(
    wavefunction,
    op_blocks,
    basis_guess,
    sector_sizes,
    kept_counts,
    target_map,
    noise_numerator,
    noise_denominator,
):
    state_count = wavefunction.shape[2]
    kept_width = basis_guess.shape[2]
    ops = lax.axis_size("op")
    tile_rows = state_count // ops
    sec_index = lax.axis_index("sec")
    op_index = lax.axis_index("op")
    noise_weight = noise_numerator[0].astype(jnp.float32) / noise_denominator[0].astype(jnp.float32)
    sources = source_sectors(target_map)
    wanted_all = jnp.take(sources, sec_index, axis=1)
    wanted = jnp.take(wanted_all, op_index)
    places = place_of(wanted_all, sec_index)
    states = jnp.arange(state_count, dtype=jnp.int32)
    own_size = jnp.take(sector_sizes, sec_index)
    own_kept = jnp.take(kept_counts, sec_index)
    own_mask = states < own_size
    source_mask = states < jnp.take(sector_sizes, wanted)
    zero_half = jnp.zeros((), jnp.bfloat16)
    own_all = lax.all_gather(wavefunction[0], "op", axis=0, tiled=True)
    moved = fetch_pieces(wavefunction[0], places)
    moved = jnp.where(source_mask[None, :], moved, zero_half)
    blocks = op_blocks[0, 0]
    perturbed = jnp.dot(moved, blocks, preferred_element_type=jnp.float32).astype(jnp.bfloat16)
    guess_rows = jnp.where(own_mask[:, None], basis_guess[0], zero_half)
    proj = noise_weight * jnp.dot(perturbed, guess_rows, preferred_element_type=jnp.float32)
    proj_high, proj_low = in_halves(proj)
    own_all = jnp.where(own_mask[None, :], own_all, zero_half)
    own_columns = lax.dynamic_slice_in_dim(own_all, op_index * tile_rows, tile_rows, 1)
    own_high, own_low = in_halves(
        jnp.dot(own_all, guess_rows, preferred_element_type=jnp.float32)
    )
    own_image = from_left(own_columns, own_high, own_low)
    scalars = jnp.stack([own_kept, op_index])
    row_ids = op_index * tile_rows + jnp.arange(tile_rows, dtype=jnp.int32)
    row_mask = row_ids < own_size
    col_mask = jnp.arange(kept_width, dtype=jnp.int32) < own_kept
    cuts = list(zip(CUTS[:-1], CUTS[1:]))
    images = []
    sums = []
    for lo, hi in cuts:
        part = from_left(perturbed, proj_high[:, lo:hi], proj_low[:, lo:hi]).astype(jnp.bfloat16)
        tiles = lax.all_to_all(part.reshape(ops, tile_rows, hi - lo), "op", 0, 0, tiled=True)
        sums.append(jnp.sum(tiles.astype(jnp.float32), axis=0) + own_image[:, lo:hi])
    for (lo, hi), total in zip(cuts, sums):
        image = jnp.where(row_mask[:, None] & col_mask[None, lo:hi], total, jnp.float32(0.0))
        images.append(from_everyone(image, "op").reshape(state_count, hi - lo))
    before, kept_tiles, mapped, fetched = [], [], [], []
    for (lo, hi), image in zip(cuts, images):
        half, tile_half, kept_tile, q = orthonormal(image, before, lo, scalars, tile_rows)
        before.append(q)
        kept_tiles.append(kept_tile)
        fetched.append(fetch_pieces(tile_half, places))
        mapped.append(
            jnp.dot(blocks, half, preferred_element_type=jnp.float32).astype(jnp.bfloat16)
        )
    mapped = jnp.concatenate(mapped, axis=1)
    rotated = jnp.concatenate(
        [
            lax.dot_general(
                source, mapped, (((0,), (0,)), ((), ())), preferred_element_type=jnp.float32
            )
            for source in fetched
        ],
        axis=0,
    )
    return (jnp.concatenate(kept_tiles, axis=1)[None], rotated[None, None])


def solution(mesh):
    placed = (
        P("sec", "op", None),
        P("op", "sec", None, None),
        P("sec", None, None),
        P(),
        P(),
        P(),
        P(),
        P(),
    )
    return jax.shard_map(
        body,
        mesh=mesh,
        in_specs=placed,
        out_specs=(P("sec", "op", None), P("op", "sec", None, None)),
        check_vma=False,
    )
```

```python
import jax
import jax.numpy as jnp
from jax import lax
from jax.experimental import pallas as pl
from jax.experimental.pallas import tpu as pltpu
from jax.sharding import PartitionSpec as P

HIGHEST = lax.Precision.HIGHEST
LANE = 128
CUTS = (0, 512)


def dot(a, b, ca, cb):
    return lax.dot_general(
        a, b, (((ca,), (cb,)), ((), ())), precision=HIGHEST, preferred_element_type=jnp.float32
    )


def dot3(a, b, ca, cb):
    dims = (((ca,), (cb,)), ((), ()))
    a_high, b_high = a.astype(jnp.bfloat16), b.astype(jnp.bfloat16)
    a_low = (a - a_high.astype(jnp.float32)).astype(jnp.bfloat16)
    b_low = (b - b_high.astype(jnp.float32)).astype(jnp.bfloat16)
    return (
        lax.dot_general(a_low, b_high, dims, preferred_element_type=jnp.float32)
        + lax.dot_general(a_high, b_low, dims, preferred_element_type=jnp.float32)
        + lax.dot_general(a_high, b_high, dims, preferred_element_type=jnp.float32)
    )


def factor_block(block):
    n = LANE
    sub = lax.broadcasted_iota(jnp.int32, (8, LANE), 0)
    lane = lax.broadcasted_iota(jnp.int32, (8, LANE), 1)
    groups = n // 8
    per = 4
    rows = [block[8 * g:8 * g + 8, :] for g in range(groups)]
    aug = [jnp.where(lane == sub + 8 * g, 1.0, 0.0).astype(jnp.float32) for g in range(groups)]
    out = []
    for s in range(0, groups, per):
        done_r, done_w = [], []
        for g in range(s, s + per):
            v, w = rows[g], aug[g]
            cols = [jnp.broadcast_to(v[:, 8 * g + j:8 * g + j + 1], (8, LANE)) for j in range(8)]
            e = {(i, j): jnp.broadcast_to(cols[j][i:i + 1, :], (8, LANE)) for j in range(8) for i in range(j, 8)}
            low, m = {}, {}
            for j in range(8):
                r = lax.rsqrt(e[j, j])
                m[j, j] = r
                for c in range(j):
                    m[j, c] = m[j, c] * r
                for i in range(j + 1, 8):
                    low[i, j] = e[i, j] * r
                for k in range(j + 1, 8):
                    for i in range(k, 8):
                        e[i, k] = e[i, k] - low[i, j] * low[k, j]
                for i in range(j + 1, 8):
                    for c in range(j + 1):
                        t = low[i, j] * m[j, c]
                        m[i, c] = m[i, c] - t if (i, c) in m else -t
            rv = rw = None
            mcols = []
            for j in range(8):
                mc = jnp.zeros((8, LANE), jnp.float32)
                for i in range(j, 8):
                    mc = jnp.where(sub == i, m[i, j], mc)
                tv = mc * jnp.broadcast_to(v[j:j + 1, :], (8, LANE))
                tw = mc * jnp.broadcast_to(w[j:j + 1, :], (8, LANE))
                rv = tv if rv is None else rv + tv
                rw = tw if rw is None else rw + tw
            out.append(rw)
            done_r.append(rv)
            done_w.append(rw)
            if g + 1 < s + per:
                rvb = [jnp.broadcast_to(rv[j:j + 1, :], (8, LANE)) for j in range(8)]
                rwb = [jnp.broadcast_to(rw[j:j + 1, :], (8, LANE)) for j in range(8)]
                for h in range(g + 1, s + per):
                    raw = [jnp.broadcast_to(rows[h][:, 8 * g + j:8 * g + j + 1], (8, LANE)) for j in range(8)]
                    nv, nw = rows[h], aug[h]
                    for i in range(8):
                        f = raw[0] * m[i, 0]
                        for k in range(1, i + 1):
                            f = f + raw[k] * m[i, k]
                        nv = nv - f * rvb[i]
                        nw = nw - f * rwb[i]
                    rows[h], aug[h] = nv, nw
        if s + per < groups:
            left = jnp.concatenate(done_r, axis=0)
            both = jnp.concatenate([left, jnp.concatenate(done_w, axis=0)], axis=1)
            rest = 8 * (s + per)
            delta = dot(left, both, 0, 0)
            for h in range(s + per, groups):
                rows[h] = rows[h] - delta[8 * h:8 * h + 8, :LANE]
                aug[h] = aug[h] - delta[8 * h:8 * h + 8, LANE:]
    return jnp.concatenate(out, axis=0)


def basis_kernel(offset, scalars_ref, image_ref, *refs):
    count = len(refs) - 6
    before = refs[:count]
    half_ref, tile_half_ref, kept_ref, q_ref, a_ref, t_ref = refs[count:]
    rows, width = image_ref.shape
    kept, own = scalars_ref[0], scalars_ref[1]
    if before:
        t_ref[...] = image_ref[...]
        for earlier in before:
            t_ref[...] = t_ref[...] - dot(
                earlier[...], dot(earlier[...], image_ref[...], 0, 0), 1, 0
            )
    else:
        t_ref[...] = image_ref[...]
    r_i = lax.broadcasted_iota(jnp.int32, (width, width), 0)
    c_i = lax.broadcasted_iota(jnp.int32, (width, width), 1)
    ones = jnp.where((r_i == c_i) & (c_i + offset >= kept), 1.0, 0.0)
    for lo in range(0, width, LANE):
        hi = lo + LANE
        a_ref[lo:hi, lo:] = dot3(t_ref[:, lo:hi], t_ref[:, lo:], 0, 0) + ones[lo:hi, lo:]
    for lo in range(0, width, LANE):
        hi = lo + LANE
        inv = factor_block(a_ref[lo:hi, lo:hi])
        t = t_ref[:, lo:hi]
        if lo:
            t = t - dot3(q_ref[:, :lo], a_ref[:lo, lo:hi], 1, 0)
        q = dot3(t, inv, 1, 1)
        q_ref[:, lo:hi] = q
        half_ref[:, lo:hi] = q.astype(jnp.bfloat16)
        if hi < width:
            r = dot(inv, a_ref[lo:hi, hi:], 1, 0)
            a_ref[lo:hi, hi:] = r
            for c in range(hi, width, LANE):
                a_ref[c : c + LANE, c:] = a_ref[c : c + LANE, c:] - dot(
                    r[:, c - hi : c - hi + LANE], r[:, c - hi :], 0, 0
                )
    tile = kept_ref.shape[0]
    mine = q_ref[pl.ds(pl.multiple_of(own * tile, tile), tile), :]
    tile_half_ref[...] = mine.astype(jnp.bfloat16)
    kept_ref[...] = mine * float(rows) ** 0.5


def orthonormal(image, before, offset, scalars, tile):
    rows, width = image.shape
    vmem = pl.BlockSpec(memory_space=pltpu.VMEM)
    return pl.pallas_call(
        lambda *refs: basis_kernel(offset, *refs),
        out_shape=(
            jax.ShapeDtypeStruct((rows, width), jnp.bfloat16),
            jax.ShapeDtypeStruct((tile, width), jnp.bfloat16),
            jax.ShapeDtypeStruct((tile, width), jnp.float32),
            jax.ShapeDtypeStruct((rows, width), jnp.float32),
        ),
        in_specs=[pl.BlockSpec(memory_space=pltpu.SMEM)] + [vmem] * (1 + len(before)),
        out_specs=(vmem,) * 4,
        scratch_shapes=[
            pltpu.VMEM((width, width), jnp.float32),
            pltpu.VMEM((rows, width), jnp.float32),
        ],
        compiler_params=pltpu.CompilerParams(vmem_limit_bytes=40 << 20),
        cost_estimate=pl.CostEstimate(
            flops=40_000_000_000 * width // 512, bytes_accessed=rows * width * 12, transcendentals=0
        ),
        name="basis_%d" % offset,
    )(scalars, image, *before)


def from_everyone(value, axis):
    size = lax.axis_size(axis)
    return lax.all_to_all(
        jnp.broadcast_to(value[None], (size, *value.shape)), axis, 0, 0, tiled=True
    )


def source_sectors(target_map):
    sectors = jnp.arange(target_map.shape[1], dtype=jnp.int32)
    matches = target_map[:, :, None] == sectors[None, None, :]
    return jnp.sum(jnp.where(matches, sectors[None, :, None], 0), axis=1)


def gather_sectors(value):
    size = lax.axis_size("sec")
    other = lax.ppermute(value, "sec", [(i, i ^ 1) for i in range(size)])
    pair = jnp.stack([value, other])
    pairs = [pair] + [
        lax.ppermute(pair, "sec", [(i, (i + 2 * step) % size) for i in range(size)])
        for step in range(1, size // 2)
    ]
    return jnp.concatenate(pairs, axis=0)


def place_of(sector, own):
    chips = lax.axis_size("sec") // 2
    return (own // 2 - sector // 2 + chips) % chips * 2 + (own + sector) % 2


def fetch_pieces(own_slice, places):
    outgoing = jnp.take(gather_sectors(own_slice), places, axis=0, mode="clip")
    incoming = lax.all_to_all(outgoing, "op", 0, 0, tiled=True)
    return incoming.reshape(-1, incoming.shape[-1])


def in_halves(value):
    high = value.astype(jnp.bfloat16)
    return high, (value - high.astype(jnp.float32)).astype(jnp.bfloat16)


def from_left(left, high, low):
    return lax.dot_general(
        jnp.concatenate([left, left], axis=0),
        jnp.concatenate([high, low], axis=0),
        (((0,), (0,)), ((), ())),
        preferred_element_type=jnp.float32,
    )


def body(
    wavefunction,
    op_blocks,
    basis_guess,
    sector_sizes,
    kept_counts,
    target_map,
    noise_numerator,
    noise_denominator,
):
    state_count = wavefunction.shape[2]
    kept_width = basis_guess.shape[2]
    ops = lax.axis_size("op")
    tile_rows = state_count // ops
    sec_index = lax.axis_index("sec")
    op_index = lax.axis_index("op")
    noise_weight = noise_numerator[0].astype(jnp.float32) / noise_denominator[0].astype(jnp.float32)
    sources = source_sectors(target_map)
    wanted_all = jnp.take(sources, sec_index, axis=1)
    wanted = jnp.take(wanted_all, op_index)
    places = place_of(wanted_all, sec_index)
    states = jnp.arange(state_count, dtype=jnp.int32)
    own_size = jnp.take(sector_sizes, sec_index)
    own_kept = jnp.take(kept_counts, sec_index)
    own_mask = states < own_size
    source_mask = states < jnp.take(sector_sizes, wanted)
    zero_half = jnp.zeros((), jnp.bfloat16)
    own_rows = jnp.where(own_mask[None, :], wavefunction[0], zero_half)
    moved = fetch_pieces(wavefunction[0], places)
    moved = jnp.where(source_mask[None, :], moved, zero_half)
    blocks = op_blocks[0, 0]
    perturbed = jnp.dot(moved, blocks, preferred_element_type=jnp.float32).astype(jnp.bfloat16)
    guess_rows = jnp.where(own_mask[:, None], basis_guess[0], zero_half)
    left = jnp.concatenate([perturbed, own_rows], axis=0)
    proj = jnp.dot(left, guess_rows, preferred_element_type=jnp.float32)
    is_noise = jnp.arange(left.shape[0]) < perturbed.shape[0]
    proj_high, proj_low = in_halves(
        proj * jnp.where(is_noise, noise_weight, jnp.float32(1.0))[:, None]
    )
    scalars = jnp.stack([own_kept, op_index])
    row_ids = op_index * tile_rows + jnp.arange(tile_rows, dtype=jnp.int32)
    row_mask = row_ids < own_size
    col_mask = jnp.arange(kept_width, dtype=jnp.int32) < own_kept
    cuts = list(zip(CUTS[:-1], CUTS[1:]))
    images = []
    sums = []
    for lo, hi in cuts:
        part = from_left(left, proj_high[:, lo:hi], proj_low[:, lo:hi]).astype(jnp.bfloat16)
        tiles = lax.all_to_all(part.reshape(ops, tile_rows, hi - lo), "op", 0, 0, tiled=True)
        sums.append(jnp.sum(tiles.astype(jnp.float32), axis=0))
    for (lo, hi), total in zip(cuts, sums):
        image = jnp.where(row_mask[:, None] & col_mask[None, lo:hi], total, jnp.float32(0.0))
        images.append(from_everyone(image, "op").reshape(state_count, hi - lo))
    before, kept_tiles, mapped, fetched = [], [], [], []
    for (lo, hi), image in zip(cuts, images):
        half, tile_half, kept_tile, q = orthonormal(image, before, lo, scalars, tile_rows)
        before.append(q)
        kept_tiles.append(kept_tile)
        fetched.append(fetch_pieces(tile_half, places))
        mapped.append(
            lax.optimization_barrier(
                jnp.dot(blocks, half, preferred_element_type=jnp.float32).astype(jnp.bfloat16)
            )
        )
    mapped = jnp.concatenate(mapped, axis=1)
    rotated = jnp.concatenate(
        [
            lax.dot_general(
                source, mapped, (((0,), (0,)), ((), ())), preferred_element_type=jnp.float32
            )
            for source in fetched
        ],
        axis=0,
    )
    return (jnp.concatenate(kept_tiles, axis=1)[None], rotated[None, None])


def solution(mesh):
    placed = (
        P("sec", "op", None),
        P("op", "sec", None, None),
        P("sec", None, None),
        P(),
        P(),
        P(),
        P(),
        P(),
    )
    return jax.shard_map(
        body,
        mesh=mesh,
        in_specs=placed,
        out_specs=(P("sec", "op", None), P("op", "sec", None, None)),
        check_vma=False,
    )
```

```python
import jax
import jax.numpy as jnp
from jax import lax
from jax.experimental import pallas as pl
from jax.experimental.pallas import tpu as pltpu
from jax.sharding import PartitionSpec as P

HIGHEST = lax.Precision.HIGHEST
LANE = 128


def dot(a, b, ca, cb):
    return lax.dot_general(
        a, b, (((ca,), (cb,)), ((), ())), precision=HIGHEST, preferred_element_type=jnp.float32
    )


def dot3(a, b, ca, cb):
    dims = (((ca,), (cb,)), ((), ()))
    a_high, b_high = a.astype(jnp.bfloat16), b.astype(jnp.bfloat16)
    a_low = (a - a_high.astype(jnp.float32)).astype(jnp.bfloat16)
    b_low = (b - b_high.astype(jnp.float32)).astype(jnp.bfloat16)
    return (
        lax.dot_general(a_low, b_high, dims, preferred_element_type=jnp.float32)
        + lax.dot_general(a_high, b_low, dims, preferred_element_type=jnp.float32)
        + lax.dot_general(a_high, b_high, dims, preferred_element_type=jnp.float32)
    )


def factor_block(block):
    n = LANE
    sub = lax.broadcasted_iota(jnp.int32, (8, LANE), 0)
    lane = lax.broadcasted_iota(jnp.int32, (8, LANE), 1)
    groups = n // 8
    per = 4
    rows = [block[8 * g:8 * g + 8, :] for g in range(groups)]
    aug = [jnp.where(lane == sub + 8 * g, 1.0, 0.0).astype(jnp.float32) for g in range(groups)]
    out = []
    for s in range(0, groups, per):
        done_r, done_w = [], []
        for g in range(s, s + per):
            v, w = rows[g], aug[g]
            cols = [jnp.broadcast_to(v[:, 8 * g + j:8 * g + j + 1], (8, LANE)) for j in range(8)]
            e = {(i, j): jnp.broadcast_to(cols[j][i:i + 1, :], (8, LANE)) for j in range(8) for i in range(j, 8)}
            low, m = {}, {}
            for j in range(8):
                r = lax.rsqrt(e[j, j])
                m[j, j] = r
                for c in range(j):
                    m[j, c] = m[j, c] * r
                for i in range(j + 1, 8):
                    low[i, j] = e[i, j] * r
                for k in range(j + 1, 8):
                    for i in range(k, 8):
                        e[i, k] = e[i, k] - low[i, j] * low[k, j]
                for i in range(j + 1, 8):
                    for c in range(j + 1):
                        t = low[i, j] * m[j, c]
                        m[i, c] = m[i, c] - t if (i, c) in m else -t
            rv = rw = None
            mcols = []
            for j in range(8):
                mc = jnp.zeros((8, LANE), jnp.float32)
                for i in range(j, 8):
                    mc = jnp.where(sub == i, m[i, j], mc)
                tv = mc * jnp.broadcast_to(v[j:j + 1, :], (8, LANE))
                tw = mc * jnp.broadcast_to(w[j:j + 1, :], (8, LANE))
                rv = tv if rv is None else rv + tv
                rw = tw if rw is None else rw + tw
            out.append(rw)
            done_r.append(rv)
            done_w.append(rw)
            if g + 1 < s + per:
                rvb = [jnp.broadcast_to(rv[j:j + 1, :], (8, LANE)) for j in range(8)]
                rwb = [jnp.broadcast_to(rw[j:j + 1, :], (8, LANE)) for j in range(8)]
                for h in range(g + 1, s + per):
                    raw = [jnp.broadcast_to(rows[h][:, 8 * g + j:8 * g + j + 1], (8, LANE)) for j in range(8)]
                    nv, nw = rows[h], aug[h]
                    for i in range(8):
                        f = raw[0] * m[i, 0]
                        for k in range(1, i + 1):
                            f = f + raw[k] * m[i, k]
                        nv = nv - f * rvb[i]
                        nw = nw - f * rwb[i]
                    rows[h], aug[h] = nv, nw
        if s + per < groups:
            left = jnp.concatenate(done_r, axis=0)
            both = jnp.concatenate([left, jnp.concatenate(done_w, axis=0)], axis=1)
            rest = 8 * (s + per)
            delta = dot(left, both, 0, 0)
            for h in range(s + per, groups):
                rows[h] = rows[h] - delta[8 * h:8 * h + 8, :LANE]
                aug[h] = aug[h] - delta[8 * h:8 * h + 8, LANE:]
    return jnp.concatenate(out, axis=0)


def basis_kernel(scalars_ref, *refs):
    blocks, (half_ref, tile_half_ref, kept_ref, q_ref, a_ref, t_ref) = refs[:-6], refs[-6:]
    rows, width = t_ref.shape
    kept, own = scalars_ref[0], scalars_ref[1]
    for b, block in enumerate(blocks):
        t_ref[:, b * LANE : (b + 1) * LANE] = block[...]
    r_i = lax.broadcasted_iota(jnp.int32, (width, width), 0)
    c_i = lax.broadcasted_iota(jnp.int32, (width, width), 1)
    ones = jnp.where((r_i == c_i) & (c_i >= kept), 1.0, 0.0)
    for lo in range(0, width, LANE):
        hi = lo + LANE
        a_ref[lo:hi, lo:] = dot3(t_ref[:, lo:hi], t_ref[:, lo:], 0, 0) + ones[lo:hi, lo:]
    for lo in range(0, width, LANE):
        hi = lo + LANE
        inv = factor_block(a_ref[lo:hi, lo:hi])
        t = t_ref[:, lo:hi]
        if lo:
            t = t - dot3(q_ref[:, :lo], a_ref[:lo, lo:hi], 1, 0)
        q = dot3(t, inv, 1, 1)
        q_ref[:, lo:hi] = q
        half_ref[:, lo:hi] = q.astype(jnp.bfloat16)
        if hi < width:
            r = dot(inv, a_ref[lo:hi, hi:], 1, 0)
            a_ref[lo:hi, hi:] = r
            for c in range(hi, width, LANE):
                a_ref[c : c + LANE, c:] = a_ref[c : c + LANE, c:] - dot(
                    r[:, c - hi : c - hi + LANE], r[:, c - hi :], 0, 0
                )
    tile = kept_ref.shape[0]
    mine = q_ref[pl.ds(pl.multiple_of(own * tile, tile), tile), :]
    tile_half_ref[...] = mine.astype(jnp.bfloat16)
    kept_ref[...] = mine * float(rows) ** 0.5


def orthonormal(blocks, scalars, tile):
    rows, width = blocks[0].shape[0], len(blocks) * LANE
    vmem = pl.BlockSpec(memory_space=pltpu.VMEM)
    return pl.pallas_call(
        basis_kernel,
        out_shape=(
            jax.ShapeDtypeStruct((rows, width), jnp.bfloat16),
            jax.ShapeDtypeStruct((tile, width), jnp.bfloat16),
            jax.ShapeDtypeStruct((tile, width), jnp.float32),
        ),
        in_specs=[pl.BlockSpec(memory_space=pltpu.SMEM)] + [vmem] * len(blocks),
        out_specs=(vmem,) * 3,
        scratch_shapes=[
            pltpu.VMEM((rows, width), jnp.float32),
            pltpu.VMEM((width, width), jnp.float32),
            pltpu.VMEM((rows, width), jnp.float32),
        ],
        compiler_params=pltpu.CompilerParams(vmem_limit_bytes=40 << 20),
        cost_estimate=pl.CostEstimate(
            flops=5_000_000_000, bytes_accessed=rows * width * 6, transcendentals=0
        ),
        name="orthonormal",
    )(scalars, *blocks)


def from_everyone(value, axis):
    size = lax.axis_size(axis)
    return lax.all_to_all(
        jnp.broadcast_to(value[None], (size, *value.shape)), axis, 0, 0, tiled=True
    )


def gathered_rows(tile):
    rows, width = tile.shape
    top = jnp.max(jnp.abs(tile))
    power = jnp.floor(jnp.log2(jnp.maximum(top, jnp.float32(1e-30))))
    scaled = (tile * jnp.exp2(12.0 - power)).astype(jnp.float16)
    sent = jnp.concatenate(
        [scaled[:, lo : lo + LANE] for lo in range(0, width, LANE)]
        + [jnp.full((16, LANE), power, jnp.float32).astype(jnp.float16)],
        axis=0,
    )
    got = from_everyone(sent, "op")
    end = width // LANE * rows
    scale = jnp.exp2(got[:, end : end + 1, :1].astype(jnp.float32) - 12.0)
    return [
        (got[:, lo : lo + rows].astype(jnp.float32) * scale).reshape(-1, LANE)
        for lo in range(0, end, rows)
    ]


def source_sectors(target_map):
    sectors = jnp.arange(target_map.shape[1], dtype=jnp.int32)
    matches = target_map[:, :, None] == sectors[None, None, :]
    return jnp.sum(jnp.where(matches, sectors[None, :, None], 0), axis=1)


def gather_sectors(value):
    size = lax.axis_size("sec")
    other = lax.ppermute(value, "sec", [(i, i ^ 1) for i in range(size)])
    pair = jnp.stack([value, other])
    pairs = [pair] + [
        lax.ppermute(pair, "sec", [(i, (i + 2 * step) % size) for i in range(size)])
        for step in range(1, size // 2)
    ]
    return jnp.concatenate(pairs, axis=0)


def place_of(sector, own):
    chips = lax.axis_size("sec") // 2
    return (own // 2 - sector // 2 + chips) % chips * 2 + (own + sector) % 2


def fetch_pieces(own_slice, places):
    outgoing = jnp.take(gather_sectors(own_slice), places, axis=0, mode="clip")
    incoming = lax.all_to_all(outgoing, "op", 0, 0, tiled=True)
    return incoming.reshape(-1, incoming.shape[-1])


def in_halves(value):
    high = value.astype(jnp.bfloat16)
    return high, (value - high.astype(jnp.float32)).astype(jnp.bfloat16)


def from_left(left, high, low):
    return lax.dot_general(
        jnp.concatenate([left, left], axis=0),
        jnp.concatenate([high, low], axis=0),
        (((0,), (0,)), ((), ())),
        preferred_element_type=jnp.float32,
    )


def body(
    wavefunction,
    op_blocks,
    basis_guess,
    sector_sizes,
    kept_counts,
    target_map,
    noise_numerator,
    noise_denominator,
):
    state_count = wavefunction.shape[2]
    kept_width = basis_guess.shape[2]
    ops = lax.axis_size("op")
    tile_rows = state_count // ops
    sec_index = lax.axis_index("sec")
    op_index = lax.axis_index("op")
    noise_weight = noise_numerator[0].astype(jnp.float32) / noise_denominator[0].astype(jnp.float32)
    sources = source_sectors(target_map)
    wanted_all = jnp.take(sources, sec_index, axis=1)
    wanted = jnp.take(wanted_all, op_index)
    places = place_of(wanted_all, sec_index)
    states = jnp.arange(state_count, dtype=jnp.int32)
    own_size = jnp.take(sector_sizes, sec_index)
    own_kept = jnp.take(kept_counts, sec_index)
    own_mask = states < own_size
    source_mask = states < jnp.take(sector_sizes, wanted)
    zero_half = jnp.zeros((), jnp.bfloat16)
    own_rows = jnp.where(own_mask[None, :], wavefunction[0], zero_half)
    moved = fetch_pieces(wavefunction[0], places)
    moved = jnp.where(source_mask[None, :], moved, zero_half)
    blocks = op_blocks[0, 0]
    perturbed = jnp.dot(moved, blocks, preferred_element_type=jnp.float32).astype(jnp.bfloat16)
    guess_rows = jnp.where(own_mask[:, None], basis_guess[0], zero_half)
    left = jnp.concatenate([perturbed, own_rows], axis=0)
    proj = jnp.dot(left, guess_rows, preferred_element_type=jnp.float32)
    is_noise = jnp.arange(left.shape[0]) < perturbed.shape[0]
    proj_high, proj_low = in_halves(
        proj * jnp.where(is_noise, noise_weight, jnp.float32(1.0))[:, None]
    )
    scalars = jnp.stack([own_kept, op_index])
    row_ids = op_index * tile_rows + jnp.arange(tile_rows, dtype=jnp.int32)
    row_mask = row_ids < own_size
    col_mask = jnp.arange(kept_width, dtype=jnp.int32) < own_kept
    part = from_left(left, proj_high, proj_low).astype(jnp.bfloat16)
    tiles = lax.all_to_all(part.reshape(ops, tile_rows, kept_width), "op", 0, 0, tiled=True)
    image = jnp.where(
        row_mask[:, None] & col_mask[None, :],
        jnp.sum(tiles.astype(jnp.float32), axis=0),
        jnp.float32(0.0),
    )
    half, tile_half, kept_tile = orthonormal(gathered_rows(image), scalars, tile_rows)
    mapped = lax.optimization_barrier(
        jnp.dot(blocks, half, preferred_element_type=jnp.float32).astype(jnp.bfloat16)
    )
    source_basis = fetch_pieces(tile_half, places)
    rotated = lax.dot_general(
        source_basis, mapped, (((0,), (0,)), ((), ())), preferred_element_type=jnp.float32
    )
    return (kept_tile[None], rotated[None, None])


def solution(mesh):
    placed = (
        P("sec", "op", None),
        P("op", "sec", None, None),
        P("sec", None, None),
        P(),
        P(),
        P(),
        P(),
        P(),
    )
    return jax.shard_map(
        body,
        mesh=mesh,
        in_specs=placed,
        out_specs=(P("sec", "op", None), P("op", "sec", None, None)),
        check_vma=False,
    )
```

```python
import functools

import jax
import jax.numpy as jnp
from jax import lax
from jax.experimental import pallas as pl
from jax.experimental.pallas import tpu as pltpu
from jax.sharding import PartitionSpec as P

LANE = 128


def dot3(a, b, ca, cb):
    dims = (((ca,), (cb,)), ((), ()))
    a_high, b_high = a.astype(jnp.bfloat16), b.astype(jnp.bfloat16)
    a_low = (a - a_high.astype(jnp.float32)).astype(jnp.bfloat16)
    b_low = (b - b_high.astype(jnp.float32)).astype(jnp.bfloat16)
    if a.shape[ca] < 2 * LANE:
        return lax.dot_general(
            jnp.concatenate([a_low, a_high, a_high], axis=ca),
            jnp.concatenate([b_high, b_low, b_high], axis=cb),
            dims,
            preferred_element_type=jnp.float32,
        )
    return (
        lax.dot_general(a_low, b_high, dims, preferred_element_type=jnp.float32)
        + lax.dot_general(a_high, b_low, dims, preferred_element_type=jnp.float32)
        + lax.dot_general(a_high, b_high, dims, preferred_element_type=jnp.float32)
    )


def total(terms):
    while len(terms) > 1:
        terms = [sum(terms[i : i + 2][1:], terms[i]) for i in range(0, len(terms), 2)]
    return terms[0]


def factor_block(block):
    n = LANE
    sub = lax.broadcasted_iota(jnp.int32, (8, LANE), 0)
    lane = lax.broadcasted_iota(jnp.int32, (8, LANE), 1)
    groups = n // 8
    per = 4
    rows = [block[8 * g:8 * g + 8, :] for g in range(groups)]
    aug = [jnp.where(lane == sub + 8 * g, 1.0, 0.0).astype(jnp.float32) for g in range(groups)]
    out = []
    for s in range(0, groups, per):
        done_r, done_w = [], []
        for g in range(s, s + per):
            v, w = rows[g], aug[g]
            cols = [jnp.broadcast_to(v[:, 8 * g + j:8 * g + j + 1], (8, LANE)) for j in range(8)]
            e = {(i, j): jnp.broadcast_to(cols[j][i:i + 1, :], (8, LANE)) for j in range(8) for i in range(j, 8)}
            low, m = {}, {}
            for j in range(8):
                r = lax.rsqrt(e[j, j])
                m[j, j] = r
                for c in range(j):
                    m[j, c] = m[j, c] * r
                for i in range(j + 1, 8):
                    low[i, j] = e[i, j] * r
                for k in range(j + 1, 8):
                    for i in range(k, 8):
                        e[i, k] = e[i, k] - low[i, j] * low[k, j]
                for i in range(j + 1, 8):
                    for c in range(j + 1):
                        t = low[i, j] * m[j, c]
                        m[i, c] = m[i, c] - t if (i, c) in m else -t
            tvs, tws = [], []
            mcols = []
            for j in range(8):
                mc = jnp.zeros((8, LANE), jnp.float32)
                for i in range(j, 8):
                    mc = jnp.where(sub == i, m[i, j], mc)
                tv = mc * jnp.broadcast_to(v[j:j + 1, :], (8, LANE))
                tw = mc * jnp.broadcast_to(w[j:j + 1, :], (8, LANE))
                tvs.append(tv)
                tws.append(tw)
            rv, rw = total(tvs), total(tws)
            out.append(rw)
            done_r.append(rv)
            done_w.append(rw)
            if g + 1 < s + per:
                rvb = [jnp.broadcast_to(rv[j:j + 1, :], (8, LANE)) for j in range(8)]
                rwb = [jnp.broadcast_to(rw[j:j + 1, :], (8, LANE)) for j in range(8)]
                for h in range(g + 1, s + per):
                    raw = [jnp.broadcast_to(rows[h][:, 8 * g + j:8 * g + j + 1], (8, LANE)) for j in range(8)]
                    nv, nw, subs_v, subs_w = rows[h], aug[h], [], []
                    for i in range(8):
                        f = total([raw[k] * m[i, k] for k in range(i + 1)])
                        subs_v.append(f * rvb[i])
                        subs_w.append(f * rwb[i])
                    rows[h] = nv - total(subs_v)
                    aug[h] = nw - total(subs_w)
        if s + per < groups:
            left = jnp.concatenate(done_r, axis=0)
            both = jnp.concatenate([left, jnp.concatenate(done_w, axis=0)], axis=1)
            rest = 8 * (s + per)
            delta = dot3(left, both, 0, 0)
            for h in range(s + per, groups):
                rows[h] = rows[h] - delta[8 * h:8 * h + 8, :LANE]
                aug[h] = aug[h] - delta[8 * h:8 * h + 8, LANE:]
    return jnp.concatenate(out, axis=0)


def basis_kernel(first, scalars_ref, *refs):
    if first:
        before_ref, given_ref = refs[:2]
        blocks, (half_ref, kept_ref, q_ref, a_ref) = refs[2:-4], refs[-4:]
        a_ref[first:, first:] = given_ref[first:, first:]
    else:
        blocks, (half_ref, kept_ref, q_ref, a_ref, t_ref) = refs[:-5], refs[-5:]
    rows, count = half_ref.shape
    width = a_ref.shape[0]
    kept, own = scalars_ref[0], scalars_ref[1]
    if not first:
        for b, block in enumerate(blocks):
            t_ref[:, b * LANE : (b + 1) * LANE] = block[...]
        r_i = lax.broadcasted_iota(jnp.int32, (width, width), 0)
        c_i = lax.broadcasted_iota(jnp.int32, (width, width), 1)
        ones = jnp.where((r_i == c_i) & (c_i >= kept), 1.0, 0.0)
        for lo in range(0, width, LANE):
            hi = lo + LANE
            a_ref[lo:hi, lo:] = dot3(t_ref[:, lo:hi], t_ref[:, lo:], 0, 0) + ones[lo:hi, lo:]
    for lo in range(first, first + count, LANE):
        hi, at = lo + LANE, lo - first
        inv = factor_block(a_ref[lo:hi, lo:hi])
        t = blocks[at // LANE][...]
        if first:
            t = t - dot3(before_ref[...], given_ref[:first, lo:hi], 1, 0)
        if at:
            t = t - dot3(q_ref[:, :at], a_ref[first:lo, lo:hi], 1, 0)
        q = dot3(t, inv, 1, 1)
        q_ref[:, at : at + LANE] = q
        half_ref[:, at : at + LANE] = q.astype(jnp.bfloat16)
        if hi < width:
            r = dot3(inv, a_ref[lo:hi, hi:], 1, 0)
            a_ref[lo:hi, hi:] = r
            for c in range(hi, width, LANE):
                a_ref[c : c + LANE, c:] = a_ref[c : c + LANE, c:] - dot3(
                    r[:, c - hi : c - hi + LANE], r[:, c - hi :], 0, 0
                )
    tile = kept_ref.shape[0]
    mine = q_ref[pl.ds(pl.multiple_of(own * tile, tile), tile), :]
    kept_ref[...] = mine * float(rows) ** 0.5


def orthonormal(first, count, blocks, scalars, tile, state=()):
    rows = blocks[0].shape[0]
    width = state[1].shape[0] if state else len(blocks) * LANE
    vmem = pl.BlockSpec(memory_space=pltpu.VMEM)
    shared = (
        jax.ShapeDtypeStruct((rows, count), jnp.float32),
        jax.ShapeDtypeStruct((width, width), jnp.float32),
    )
    scratch = [pltpu.VMEM(item.shape, item.dtype) for item in shared]
    return pl.pallas_call(
        functools.partial(basis_kernel, first),
        out_shape=(
            jax.ShapeDtypeStruct((rows, count), jnp.bfloat16),
            jax.ShapeDtypeStruct((tile, count), jnp.float32),
        )
        + (() if state else shared),
        in_specs=[pl.BlockSpec(memory_space=pltpu.SMEM)] + [vmem] * (len(blocks) + len(state)),
        out_specs=(vmem,) * (2 if state else 4),
        scratch_shapes=scratch if state else [pltpu.VMEM((rows, width), jnp.float32)],
        compiler_params=pltpu.CompilerParams(vmem_limit_bytes=14 << 20),
        cost_estimate=pl.CostEstimate(
            flops=10_000_000_000, bytes_accessed=rows * width * 6, transcendentals=0
        ),
        name="orthonormal_%d" % first,
    )(scalars, *state, *blocks)


def from_everyone(value, axis):
    size = lax.axis_size(axis)
    return lax.all_to_all(
        jnp.broadcast_to(value[None], (size, *value.shape)), axis, 0, 0, tiled=True
    )


def gathered_rows(tile):
    rows, width = tile.shape
    top = jnp.max(jnp.abs(tile))
    power = jnp.floor(jnp.log2(jnp.maximum(top, jnp.float32(1e-30))))
    scaled = (tile * jnp.exp2(12.0 - power)).astype(jnp.float16)
    sent = jnp.concatenate(
        [scaled[:, lo : lo + LANE] for lo in range(0, width, LANE)]
        + [jnp.full((8, LANE), power, jnp.float32).astype(jnp.float16)],
        axis=0,
    )
    got = from_everyone(sent, "op")
    end = width // LANE * rows
    scale = jnp.exp2(got[:, end : end + 1, :1].astype(jnp.float32) - 12.0)
    return [
        (got[:, lo : lo + rows].astype(jnp.float32) * scale).reshape(-1, LANE)
        for lo in range(0, end, rows)
    ]


def source_sectors(target_map):
    sectors = jnp.arange(target_map.shape[1], dtype=jnp.int32)
    matches = target_map[:, :, None] == sectors[None, None, :]
    return jnp.sum(jnp.where(matches, sectors[None, :, None], 0), axis=1)


def gather_sectors(value):
    size = lax.axis_size("sec")
    chips = jnp.stack(
        [value]
        + [
            lax.ppermute(value, "sec", [(i, (i + 2 * step) % size) for i in range(size)])
            for step in range(1, size // 2)
        ]
    )
    other = lax.ppermute(chips, "sec", [(i, i ^ 1) for i in range(size)])
    return jnp.concatenate([chips, other], axis=0)


def place_of(sector, own):
    chips = lax.axis_size("sec") // 2
    return (own // 2 - sector // 2 + chips) % chips + (own + sector) % 2 * chips


def fetch_pieces(own_slice, places):
    outgoing = jnp.take(gather_sectors(own_slice), places, axis=0, mode="clip")
    incoming = lax.all_to_all(outgoing, "op", 0, 0, tiled=True)
    return incoming.reshape(-1, incoming.shape[-1])


def exchanged_sectors(values, wanted):
    size = lax.axis_size("sec")
    picked = []
    for value in values:
        if picked:
            value, picked[-1] = lax.optimization_barrier((value, picked[-1]))
        pieces = value.reshape(size, value.shape[0] // size, value.shape[1])
        spread = lax.all_to_all(pieces, "sec", 0, 0, tiled=True)
        picked.append(jnp.take(spread, wanted, axis=0, mode="clip"))
    picked = jnp.concatenate(picked, axis=2)
    got = lax.all_to_all(picked, "sec", 0, 0, tiled=True)
    return got.reshape(-1, got.shape[2])


def in_halves(value):
    high = value.astype(jnp.bfloat16)
    return high, (value - high.astype(jnp.float32)).astype(jnp.bfloat16)


def from_left(left, high, low):
    return lax.dot_general(
        jnp.concatenate([left, left], axis=0),
        jnp.concatenate([high, low], axis=0),
        (((0,), (0,)), ((), ())),
        preferred_element_type=jnp.float32,
    )


def body(
    wavefunction,
    op_blocks,
    basis_guess,
    sector_sizes,
    kept_counts,
    target_map,
    noise_numerator,
    noise_denominator,
):
    state_count = wavefunction.shape[2]
    kept_width = basis_guess.shape[2]
    ops = lax.axis_size("op")
    tile_rows = state_count // ops
    sec_index = lax.axis_index("sec")
    op_index = lax.axis_index("op")
    noise_weight = noise_numerator[0].astype(jnp.float32) / noise_denominator[0].astype(jnp.float32)
    sources = source_sectors(target_map)
    wanted_all = jnp.take(sources, sec_index, axis=1)
    wanted = jnp.take(wanted_all, op_index)
    places = place_of(wanted_all, sec_index)
    states = jnp.arange(state_count, dtype=jnp.int32)
    own_size = jnp.take(sector_sizes, sec_index)
    own_kept = jnp.take(kept_counts, sec_index)
    own_mask = states < own_size
    source_mask = states < jnp.take(sector_sizes, wanted)
    zero_half = jnp.zeros((), jnp.bfloat16)
    own_rows = jnp.where(own_mask[None, :], wavefunction[0], zero_half)
    moved = fetch_pieces(wavefunction[0], places)
    moved = jnp.where(source_mask[None, :], moved, zero_half)
    blocks = op_blocks[0, 0]
    perturbed = jnp.dot(moved, blocks, preferred_element_type=jnp.float32).astype(jnp.bfloat16)
    guess_rows = jnp.where(own_mask[:, None], basis_guess[0], zero_half)
    left = jnp.concatenate([perturbed, own_rows], axis=0)
    proj = jnp.dot(left, guess_rows, preferred_element_type=jnp.float32)
    is_noise = jnp.arange(left.shape[0]) < perturbed.shape[0]
    proj_high, proj_low = in_halves(
        proj * jnp.where(is_noise, noise_weight, jnp.float32(1.0))[:, None]
    )
    scalars = jnp.stack([own_kept, op_index])
    row_ids = op_index * tile_rows + jnp.arange(tile_rows, dtype=jnp.int32)
    row_mask = row_ids < own_size
    col_mask = jnp.arange(kept_width, dtype=jnp.int32) < own_kept
    part = from_left(left, proj_high, proj_low).astype(jnp.bfloat16)
    tiles = lax.all_to_all(part.reshape(ops, tile_rows, kept_width), "op", 0, 0, tiled=True)
    image = jnp.where(
        row_mask[:, None] & col_mask[None, :],
        jnp.sum(tiles.astype(jnp.float32), axis=0),
        jnp.float32(0.0),
    )
    images = gathered_rows(image)
    first = kept_width // 2
    half_a, kept_a, *state = orthonormal(0, first, images, scalars, tile_rows)
    half_b, kept_b = orthonormal(
        first, kept_width - first, images[first // LANE :], scalars, tile_rows, state
    )
    kept_tile = jnp.concatenate([kept_a, kept_b], axis=1)
    source_basis = exchanged_sectors(
        (half_a, half_b), lax.dynamic_index_in_dim(sources, op_index, 0, False)
    )
    mapped = lax.optimization_barrier(
        jnp.dot(
            blocks,
            jnp.concatenate([half_a, half_b], axis=1),
            preferred_element_type=jnp.float32,
        ).astype(jnp.bfloat16)
    )
    rotated = lax.dot_general(
        source_basis, mapped, (((0,), (0,)), ((), ())), preferred_element_type=jnp.float32
    )
    return (kept_tile[None], rotated[None, None])


def solution(mesh):
    placed = (
        P("sec", "op", None),
        P("op", "sec", None, None),
        P("sec", None, None),
        P(),
        P(),
        P(),
        P(),
        P(),
    )
    return jax.shard_map(
        body,
        mesh=mesh,
        in_specs=placed,
        out_specs=(P("sec", "op", None), P("op", "sec", None, None)),
        check_vma=False,
    )
```
